128 devices in a mesh: grp: 4 (over z_lo, core), dev: 32 (over z_hi, x, y).
Axes of the slice: x: 4, y: 4, z: 4 (z_hi: 2, z_lo: 2; z = z_hi * 2 + z_lo), core: 2. Of those that a mesh axis runs over, the one named last changes fastest.
Arguments:
- fine_residual: bfloat16 [4, 32, 4, 4, 24, 2, 3072], P('grp', 'dev'), may hold values from -4 to 4
- near_null: bfloat16 [4, 32, 4, 4, 2, 32, 3072], P('grp', 'dev'), may hold values from -0.375 to 0.375
- coarse_operator: bfloat16 [4, 32, 4, 4, 64, 1152], P(None, 'dev'), may hold values from -1 to 7
Outputs:
- fine_correction: bfloat16 [4, 32, 4, 4, 24, 2, 3072], P('grp', 'dev')
- coarse_residual: float32 [4, 32, 4, 4, 24, 128], P('grp', 'dev')
The draws below stay inside these ranges and needn't reach their ends.
All inputs are finite; a program needn't handle non-finite values.
Results may differ from the reference program's by a relative error of at most 0.012.
The reference program's roundings to bfloat16 on the way count: a program that leaves them out, or rounds other values in their place, can miss the bound.
Values may be sent and summed in bfloat16 or wider, within the bound.
A program may use at most 128 MiB of HBM per device.

```python
import functools
import math
import jax
import jax.numpy as jnp
from jax import lax

NVEC = 32
COARSE = 64
SPINCOL = 12
BLOCK = 256
NRHS = 24
LY = 4
LX = 4
ITERS = 3
LT = 4
LZ = 32


def draw_fine_residual(key, part):
    extent = (LT, LZ, LY, LX, NRHS, 2, SPINCOL * BLOCK)
    depth = jnp.arange(LZ, dtype=jnp.float32).reshape(1, LZ, 1, 1, 1, 1, 1) / max(LZ - 1, 1)
    former = jax.random.fold_in(key, 0)
    gradient = jnp.exp(depth * math.log(10.0))
    values = 0.12 * gradient * jax.random.normal(former, extent, jnp.float32)
    return jnp.clip(values, -4.0, 4.0).astype(jnp.bfloat16)


def draw_coarse_operator(key, part):
    rows = COARSE
    cols = 18 * COARSE
    extent = (LT, LZ, LY, LX, rows, cols)
    spread = 0.4 / math.sqrt(18.0 * COARSE)
    former, latter = jax.random.split(key)
    row_ids = lax.broadcasted_iota(jnp.int32, (rows, cols), 0)
    col_ids = lax.broadcasted_iota(jnp.int32, (rows, cols), 1)
    on_diag = (row_ids == col_ids).astype(jnp.float32)
    depth = jnp.arange(LZ, dtype=jnp.float32).reshape(1, LZ, 1, 1, 1, 1) / max(LZ - 1, 1)
    rising = 1.0 + 2.0 * depth
    jitter = jnp.clip(jax.random.normal(former, extent, jnp.float32), -4.0, 4.0) * spread
    diagonal_level = jax.random.uniform(latter, (LT, LZ, LY, LX, rows, 1), jnp.float32, 1.0, 2.0)
    return (jitter + rising * diagonal_level * on_diag).astype(jnp.bfloat16)


def steps_of(rng, shape, cuts, smallest, high):
    loudness = 1.0
    for position, blocks in cuts:
        steps = jax.random.uniform(jax.random.fold_in(jax.random.fold_in(rng, 6), position), (blocks,), jnp.float32, smallest / len(cuts), high / len(cuts))
        loudness = loudness * jnp.repeat(jnp.exp(steps), shape[position] // blocks).reshape((-1,) + (1,) * (len(shape) - 1 - position))
    return loudness


def centred(own_key, dims, width, limit, pieces=(), held_as=jnp.bfloat16):
    array = jax.random.normal(own_key, dims, jnp.float32) * width
    if len(pieces) > 0:
        array = steps_of(own_key, dims, pieces, -0.22, 0.18) * array
    return jnp.clip(array, min=-limit, max=limit).astype(held_as)


def setup_inputs(seed: int = 0) -> dict:
    arg_keys = jax.random.split(jax.random.key(seed), 4)
    return {
        "fine_residual": draw_fine_residual(jax.random.fold_in(arg_keys[3], 71), 0),
        "near_null": centred(arg_keys[1], (LT, LZ, LY, LX, 2, NVEC, SPINCOL * BLOCK), BLOCK ** -0.5, 0.375, ((0, 4), (1, 32))),
        "coarse_operator": draw_coarse_operator(jax.random.fold_in(arg_keys[3], 71), 0),
    }


def complex_columns(piece, ncoarse):
    real_part = piece[..., :ncoarse]
    imag_part = piece[..., ncoarse:]
    former = jnp.concatenate([real_part, -imag_part], axis=-1)
    latter = jnp.concatenate([imag_part, real_part], axis=-1)
    return jnp.stack([former, latter], axis=-2)


def restrict_plane(operands):
    vectors, field = operands
    middle = vectors.shape[-1] // 2
    vectors = vectors.astype(jnp.float32)
    field = field.astype(jnp.float32)
    upper = jnp.einsum("zyxpkm,zyxnqm->zyxnpqk", vectors[..., :middle], field[..., :middle])
    lower = jnp.einsum("zyxpkm,zyxnqm->zyxnpqk", vectors[..., middle:], field[..., middle:])
    joined = jnp.concatenate([upper, lower], axis=-1)
    real_part = joined[..., 0, 0, :] + joined[..., 1, 1, :]
    imag_part = joined[..., 0, 1, :] - joined[..., 1, 0, :]
    return jnp.concatenate([real_part, imag_part], axis=-1)


def coefficients(solution, first_index, last_index, ncoarse):
    real_part = solution[..., first_index:last_index]
    imag_part = solution[..., ncoarse + first_index:ncoarse + last_index]
    former = jnp.stack([real_part, -imag_part], axis=-2)
    latter = jnp.stack([imag_part, real_part], axis=-2)
    return jnp.stack([former, latter], axis=-3)


def prolong_plane(operands):
    vectors, rounded = operands
    vector_count = vectors.shape[-2]
    ncoarse = 2 * vector_count
    middle = vectors.shape[-1] // 2
    vectors = vectors.astype(jnp.float32)
    upper = jnp.einsum("zyxnqpk,zyxpkm->zyxnqm", coefficients(rounded, 0, vector_count, ncoarse).astype(jnp.float32), vectors[..., :middle])
    lower = jnp.einsum("zyxnqpk,zyxpkm->zyxnqm", coefficients(rounded, vector_count, ncoarse, ncoarse).astype(jnp.float32), vectors[..., middle:])
    return jnp.concatenate([upper, lower], axis=-1).astype(jnp.bfloat16)


def apply_plane(operands):
    blocks, columns = operands
    leading = blocks.shape[:3]
    sites_total = leading[0] * leading[1] * leading[2]
    ncoarse = blocks.shape[-2]
    blocks = blocks.reshape(sites_total, ncoarse, 9, 2 * ncoarse).astype(jnp.float32)
    columns = columns.reshape((sites_total,) + columns.shape[3:]).astype(jnp.float32)
    result = jnp.einsum("sidk,sdnqk->snqi", blocks, columns)
    return result.reshape(leading + (result.shape[1], 2 * ncoarse))


def coarse_apply(operator, vector, ncoarse):
    rounded = vector.astype(jnp.bfloat16)
    shifted = [rounded]
    for dimension in range(4):
        shifted.append(jnp.roll(rounded, -1, dimension))
        shifted.append(jnp.roll(rounded, 1, dimension))
    columns = complex_columns(jnp.stack(shifted, axis=4), ncoarse)
    return lax.map(apply_plane, (operator, columns))


def inner_terms(left, right, ncoarse):
    left_re = left[..., :ncoarse]
    left_im = left[..., ncoarse:]
    right_re = right[..., :ncoarse]
    right_im = right[..., ncoarse:]
    summed = (0, 1, 2, 3, 5)
    return jnp.stack([jnp.sum(left_re * right_re + left_im * right_im, axis=summed),
                      jnp.sum(left_re * right_im - left_im * right_re, axis=summed)])


def scaled(coef, vector, ncoarse):
    coef_real = coef[0][:, None]
    coef_imag = coef[1][:, None]
    vec_real = vector[..., :ncoarse]
    vec_imag = vector[..., ncoarse:]
    return jnp.concatenate([coef_real * vec_real - coef_imag * vec_imag,
                            coef_real * vec_imag + coef_imag * vec_real], axis=-1)


def reference(fine_residual, near_null, coarse_operator):
    ncoarse = 2 * near_null.shape[-2]
    source = lax.map(restrict_plane, (near_null, fine_residual))
    apply_fn = functools.partial(coarse_apply, coarse_operator, ncoarse=ncoarse)
    solution = jnp.zeros_like(source)
    residual = source
    directions = []
    images = []
    curvatures = []
    for iteration in range(ITERS):
        direction = residual
        product = apply_fn(direction)
        correlations = [inner_terms(earlier_q, product, ncoarse) for earlier_q in images]
        for earlier in range(iteration):
            factor = correlations[earlier] / curvatures[earlier][None, :]
            product = product - scaled(factor, images[earlier], ncoarse)
            direction = direction - scaled(factor, directions[earlier], ncoarse)
        curvature = inner_terms(product, product, ncoarse)[0]
        along = inner_terms(product, residual, ncoarse)
        step_size = along / curvature[None, :]
        solution = solution + scaled(step_size, direction, ncoarse)
        residual = residual - scaled(step_size, product, ncoarse)
        directions.append(direction)
        images.append(product)
        curvatures.append(curvature)
    rounded = solution.astype(jnp.bfloat16)
    fine_correction = lax.map(prolong_plane, (near_null, rounded))
    return fine_correction, residual
```

```python
import jax
import jax.numpy as jnp
from jax import lax
from jax.experimental import pallas as pl
from jax.experimental.pallas import tpu as pltpu
from jax.sharding import PartitionSpec as P

ITERS = 3
SITES = 16
SIDE = 4
NRHS = 24
NVEC = 64
COMP = 128
FINE = 3072
HALF = FINE // 2
GRP = 4
DEV = 32
PLANE = 16
LINE = 8
GROUPS = 4
PER = SITES // GROUPS
BF = jnp.bfloat16
F32 = jnp.float32
NT = (((1,), (1,)), ((), ()))
VMEM_LIMIT = 60 * 2**20


def lanes():
    return lax.broadcasted_iota(jnp.int32, (1, COMP), 1)


def flipped(v):
    return jnp.where(lanes() < 64, 1.0, -1.0) * pltpu.roll(v, 64, 1)


def restrict_sites(cat, first):
    even = cat[pl.ds(2 * NRHS * first, NRHS * PER, stride=2), :]
    odd = cat[pl.ds(2 * NRHS * first + 1, NRHS * PER, stride=2), :]
    re = even + pltpu.roll(odd, 96, 1)
    im = odd - pltpu.roll(even, 96, 1)
    lane = lanes()
    return jnp.where(
        lane < 32,
        re,
        jnp.where(
            lane < 64,
            pltpu.roll(re, 96, 1),
            jnp.where(lane < 96, pltpu.roll(im, 64, 1), pltpu.roll(im, 32, 1)),
        ),
    )


def coefficient_rows(c):
    lane = lanes()
    r32, r64, r96 = (pltpu.roll(c, k, 1) for k in (32, 64, 96))
    real = jnp.where(lane < 32, c, jnp.where(lane < 64, -r96, jnp.where(lane < 96, r32, -c)))
    imag = jnp.where(lane < 32, r64, jnp.where(lane < 64, r32, jnp.where(lane < 96, r96, r64)))
    return real, imag


def packed(terms):
    lane = lanes()
    out = jnp.zeros((8, COMP), F32)
    for t, values in enumerate(terms):
        total = jnp.sum(values, axis=1, keepdims=True)
        for a in range(3):
            out = jnp.where(lane == 32 * a + t, total[8 * a : 8 * a + 8], out)
    return out


def unpacked(message, t):
    return message if t == 0 else pltpu.roll(message, COMP - t, 1)


def spread(coef):
    return jnp.concatenate(
        [jnp.broadcast_to(coef[:, 32 * a : 32 * a + 1], (8, COMP)) for a in range(3)], axis=0
    )


def scale(re, im):
    re, im = spread(re), spread(im)
    return lambda v: re * v - im * flipped(v)


def site(y, x):
    return (y % SIDE) * SIDE + x % SIDE


def gcr_kernel(
    f_hbm, v_hbm, op_hbm, coef_ref, out_ref,
    fb, vb, ob, wide, cat, res, first, second, sol, prod, low, halo,
    msg1, msg2, box1, box2,
    f_sem, v_sem, o_sem, h_send, h_recv, s1_send, s1_recv, s2_send, s2_recv,
):
    g = lax.axis_index("grp")
    d = lax.axis_index("dev")
    high = d // PLANE
    place = d % PLANE
    line = high * GRP + g

    def line_peer(k):
        other = (line + k) % LINE
        return {"grp": other % GRP, "dev": (other // GRP) * PLANE + place}

    def plane_peer(k):
        return {"grp": g, "dev": high * PLANE + (place + k) % PLANE}

    halo_to = [
        {"grp": (g + GRP - 1) % GRP, "dev": d},
        {"grp": (g + 1) % GRP, "dev": d},
        {"grp": g, "dev": (d + DEV - 1) % DEV},
        {"grp": g, "dev": (d + 1) % DEV},
    ]

    copies = []
    for j in range(GROUPS):
        part = pl.ds(j * PER, PER)
        pair = (
            pltpu.make_async_copy(f_hbm.at[part], fb.at[part], f_sem.at[j]),
            pltpu.make_async_copy(v_hbm.at[part], vb.at[part], v_sem.at[j]),
        )
        for copy in pair:
            copy.start()
        copies.append(pair)
    op_copy = pltpu.make_async_copy(op_hbm.at[g], ob, o_sem)
    op_copy.start()

    barrier = pltpu.get_barrier_semaphore()
    greeted = halo_to[2:] + [line_peer(k) for k in range(1, LINE)]
    greeted += [plane_peer(k) for k in range(1, PLANE)]
    for peer in greeted:
        pl.semaphore_signal(barrier, inc=1, device_id=peer, device_id_type=pl.DeviceIdType.MESH)

    for j in range(GROUPS):
        for copy in copies[j]:
            copy.wait()
        for s in range(j * PER, j * PER + PER):
            f = fb[s].reshape(2 * NRHS, FINE)
            upper = lax.dot_general(f[:, :HALF], vb[s, :, :HALF], NT, preferred_element_type=F32)
            lower = lax.dot_general(f[:, HALF:], vb[s, :, HALF:], NT, preferred_element_type=F32)
            cat[2 * NRHS * s : 2 * NRHS * (s + 1), :] = jnp.concatenate([upper, lower], axis=1)
        block = restrict_sites(cat, j * PER).reshape(PER, NRHS, COMP)
        res[0, pl.ds(j * PER, PER)] = block
        low[0, pl.ds(j * PER, PER)] = block.astype(BF)
    pl.semaphore_wait(barrier, len(greeted))

    sends = []

    def remote(src, dst, send, recv, peer):
        copy = pltpu.make_async_remote_copy(
            src_ref=src, dst_ref=dst, send_sem=send, recv_sem=recv,
            device_id=peer, device_id_type=pl.DeviceIdType.MESH,
        )
        copy.start()
        sends.append(copy)
        return copy

    def start_halo(k):
        return [
            remote(low.at[k], halo.at[k, h], h_send.at[k, h], h_recv.at[k, h], halo_to[h])
            for h in range(4)
        ]

    def widen():
        keep = jnp.where(lanes() < 64, 1.0, -1.0).astype(BF)
        for s in range(SITES):
            for c in range(9):
                block = ob[s, :, COMP * c : COMP * (c + 1)]
                wide[s, 0:64, COMP * c : COMP * (c + 1)] = block * keep
                wide[s, 64:128, COMP * c : COMP * (c + 1)] = jnp.concatenate(
                    [block[:, 64:], block[:, :64]], axis=1
                )

    def apply_own(k):
        for y in range(SIDE):
            for x in range(SIDE):
                s = site(y, x)
                near = [site(y + 1, x), site(y - 1, x), site(y, x + 1), site(y, x - 1)]
                side = jnp.concatenate([low[k, n] for n in near], axis=1)
                prod[k, s] = lax.dot_general(
                    low[k, s], wide[s, :, :COMP], NT, preferred_element_type=F32
                ) + lax.dot_general(side, wide[s, :, 5 * COMP :], NT, preferred_element_type=F32)

    def apply_halo(k):
        for s in range(SITES):
            far = jnp.concatenate([halo[k, h, s] for h in range(4)], axis=1)
            prod[k, s] += lax.dot_general(
                far, wide[s, :, COMP : 5 * COMP], NT, preferred_element_type=F32
            )

    def total(k, terms, meanwhile):
        mine = packed(terms)
        msg1[k] = mine
        arriving = [
            remote(msg1.at[k], box1.at[k, i - 1], s1_send.at[k, i - 1], s1_recv.at[k, i - 1], line_peer(i))
            for i in range(1, LINE)
        ]
        meanwhile()
        for copy in arriving:
            copy.wait_recv()
        mine = mine + jnp.sum(box1[k], axis=0)
        msg2[k] = mine
        arriving = [
            remote(msg2.at[k], box2.at[k, i - 1], s2_send.at[k, i - 1], s2_recv.at[k, i - 1], plane_peer(i))
            for i in range(1, PLANE)
        ]
        for copy in arriving:
            copy.wait_recv()
        return mine + jnp.sum(box2[k], axis=0)

    def inner(k):
        zero = jnp.zeros((NRHS, COMP), F32)
        sums = [zero] * (3 + 4 * k)
        for s in range(SITES):
            q, r = prod[k, s], res[k, s]
            iq, ir = flipped(q), flipped(r)
            new = [q * q, q * r, q * ir]
            for j in range(k):
                e = prod[j, s]
                new += [e * q, e * iq, e * r, e * ir]
            sums = [a + b for a, b in zip(sums, new)]
        return sums

    arriving = start_halo(0)
    op_copy.wait()
    widen()
    apply_own(0)
    for copy in arriving:
        copy.wait_recv()
    apply_halo(0)
    sums = total(0, inner(0), lambda: None)
    norm0 = unpacked(sums, 0)
    a0_re, a0_im = unpacked(sums, 1) / norm0, unpacked(sums, 2) / norm0
    step = scale(a0_re, a0_im)
    for s in range(SITES):
        r = res[0, s] - step(prod[0, s])
        res[1, s] = r
        low[1, s] = r.astype(BF)

    arriving = start_halo(1)
    for s in range(SITES):
        sol[s] = step(res[0, s])
    apply_own(1)
    for copy in arriving:
        copy.wait_recv()
    apply_halo(1)
    sums = total(1, inner(1), lambda: None)
    s_re, s_im = unpacked(sums, 3), unpacked(sums, 4)
    b_re, b_im = s_re / norm0, s_im / norm0
    norm1 = unpacked(sums, 0) - (b_re * s_re + b_im * s_im)
    e_re, e_im = unpacked(sums, 5), unpacked(sums, 6)
    along_re = unpacked(sums, 1) - (b_re * e_re + b_im * e_im)
    along_im = unpacked(sums, 2) - (b_re * e_im - b_im * e_re)
    back = scale(b_re, b_im)
    step = scale(along_re / norm1, along_im / norm1)
    for s in range(SITES):
        q = prod[1, s] - back(prod[0, s])
        prod[1, s] = q
        r = res[1, s] - step(q)
        res[2, s] = r
        low[2, s] = r.astype(BF)

    arriving = start_halo(2)
    for s in range(SITES):
        p = res[1, s] - back(res[0, s])
        first[s] = p
        sol[s] += step(p)
    apply_own(2)
    for copy in arriving:
        copy.wait_recv()
    apply_halo(2)
    sums = total(2, inner(2), lambda: None)
    s_re, s_im, e_re, e_im = (unpacked(sums, 3 + i) for i in range(4))
    u_re, u_im, w_re, w_im = (unpacked(sums, 7 + i) for i in range(4))
    b_re, b_im = s_re / norm0, s_im / norm0
    c_re, c_im = u_re / norm1, u_im / norm1
    norm2 = unpacked(sums, 0) - (b_re * s_re + b_im * s_im) - (c_re * u_re + c_im * u_im)
    along_re = unpacked(sums, 1) - (b_re * e_re + b_im * e_im) - (c_re * w_re + c_im * w_im)
    along_im = unpacked(sums, 2) - (b_re * e_im - b_im * e_re) - (c_re * w_im - c_im * w_re)
    back0, back1 = scale(b_re, b_im), scale(c_re, c_im)
    step = scale(along_re / norm2, along_im / norm2)
    for s in range(SITES):
        q = prod[2, s] - back0(prod[0, s]) - back1(prod[1, s])
        out_ref[s] = res[2, s] - step(q)
        p = res[2, s] - back0(res[0, s]) - back1(first[s])
        x = sol[s] + step(p)
        real, imag = coefficient_rows(x.astype(BF).astype(F32))
        second[pl.ds(2 * NRHS * s, NRHS, stride=2), :] = real
        second[pl.ds(2 * NRHS * s + 1, NRHS, stride=2), :] = imag
        coef_ref[s] = second[2 * NRHS * s : 2 * NRHS * (s + 1), :].astype(BF)
    for copy in sends:
        copy.wait_send()


def solve(fine, vectors, operator):
    any_space = pl.BlockSpec(memory_space=pl.ANY)
    in_vmem = pl.BlockSpec(memory_space=pltpu.VMEM)
    field = (SITES, NRHS, COMP)
    dma = pltpu.SemaphoreType.DMA
    return pl.pallas_call(
        gcr_kernel,
        out_shape=(
            jax.ShapeDtypeStruct((SITES, 2 * NRHS, COMP), BF),
            jax.ShapeDtypeStruct(field, F32),
        ),
        in_specs=[any_space] * 3,
        out_specs=(in_vmem, in_vmem),
        scratch_shapes=[
            pltpu.VMEM((SITES, NRHS, 2, FINE), BF),
            pltpu.VMEM((SITES, NVEC, FINE), BF),
            pltpu.VMEM((SITES, 64, 9 * COMP), BF),
            pltpu.VMEM((SITES, 128, 9 * COMP), BF),
            pltpu.VMEM((SITES * 2 * NRHS, COMP), F32),
            pltpu.VMEM((ITERS, *field), F32),
            pltpu.VMEM(field, F32),
            pltpu.VMEM((SITES * 2 * NRHS, COMP), F32),
            pltpu.VMEM(field, F32),
            pltpu.VMEM((ITERS, *field), F32),
            pltpu.VMEM((ITERS, *field), BF),
            pltpu.VMEM((ITERS, 4, *field), BF),
            pltpu.VMEM((ITERS, 8, COMP), F32),
            pltpu.VMEM((ITERS, 8, COMP), F32),
            pltpu.VMEM((ITERS, LINE - 1, 8, COMP), F32),
            pltpu.VMEM((ITERS, PLANE - 1, 8, COMP), F32),
            dma((GROUPS,)),
            dma((GROUPS,)),
            dma,
            dma((ITERS, 4)),
            dma((ITERS, 4)),
            dma((ITERS, LINE - 1)),
            dma((ITERS, LINE - 1)),
            dma((ITERS, PLANE - 1)),
            dma((ITERS, PLANE - 1)),
        ],
        compiler_params=pltpu.CompilerParams(
            collective_id=0, has_side_effects=True, vmem_limit_bytes=VMEM_LIMIT
        ),
        name="restrict_gcr",
    )(fine, vectors, operator)


def prolong_kernel(v_hbm, coef_ref, o_hbm, yb, vb, v_sem, o_sem):
    loads, stores = [], []
    for j in range(GROUPS):
        part = pl.ds(j * PER, PER)
        loads.append(pltpu.make_async_copy(v_hbm.at[part], vb.at[part], v_sem.at[j]))
        stores.append(pltpu.make_async_copy(yb.at[part], o_hbm.at[part], o_sem.at[j]))
        loads[j].start()
    for j in range(GROUPS):
        loads[j].wait()
        for s in range(j * PER, j * PER + PER):
            c = coef_ref[s]
            upper = jnp.dot(c[:, :64], vb[s, :, :HALF], preferred_element_type=F32).astype(BF)
            lower = jnp.dot(c[:, 64:], vb[s, :, HALF:], preferred_element_type=F32).astype(BF)
            yb[s] = jnp.concatenate([upper, lower], axis=1).reshape(NRHS, 2, FINE)
        stores[j].start()
    for store in stores:
        store.wait()


def prolong(vectors, coef):
    return pl.pallas_call(
        prolong_kernel,
        out_shape=jax.ShapeDtypeStruct((SITES, NRHS, 2, FINE), BF),
        in_specs=[pl.BlockSpec(memory_space=pl.ANY), pl.BlockSpec(memory_space=pltpu.VMEM)],
        out_specs=pl.BlockSpec(memory_space=pl.ANY),
        scratch_shapes=[
            pltpu.VMEM((SITES, NRHS, 2, FINE), BF),
            pltpu.VMEM((SITES, NVEC, FINE), BF),
            pltpu.SemaphoreType.DMA((GROUPS,)),
            pltpu.SemaphoreType.DMA((GROUPS,)),
        ],
        compiler_params=pltpu.CompilerParams(vmem_limit_bytes=VMEM_LIMIT),
        name="prolong",
    )(vectors, coef)


def on_device(fine_residual, near_null, coarse_operator):
    fine = fine_residual.reshape(SITES, NRHS, 2, FINE)
    vectors = near_null.reshape(SITES, NVEC, FINE)
    operator = coarse_operator.reshape(GRP, SITES, 64, 9 * COMP)
    coef, residual = solve(fine, vectors, operator)
    fine_correction = prolong(vectors, coef)
    return (
        fine_correction.reshape(fine_residual.shape),
        residual.reshape(fine_residual.shape[:4] + (NRHS, COMP)),
    )


def solution(mesh):
    in_specs = (
        P("grp", "dev", None, None, None, None, None),
        P("grp", "dev", None, None, None, None, None),
        P(None, "dev", None, None, None, None),
    )
    out_specs = (
        P("grp", "dev", None, None, None, None, None),
        P("grp", "dev", None, None, None, None),
    )
    return jax.shard_map(
        on_device, mesh=mesh, in_specs=in_specs, out_specs=out_specs, check_vma=False
    )
```
